32 devices in a mesh: ep: 16 (over z, x, core), etp: 2 (over y).
Axes of the slice: x: 2, y: 2, z: 4, core: 2. Of those that a mesh axis runs over, the one named last changes fastest.
Arguments:
- tokens: bfloat16 [2048, 4096], P('ep', 'etp'), may hold values from -6 to 6
- grad_out: bfloat16 [2048, 4096], P('ep', 'etp'), may hold values from -1.5 to 1.5
- gates: float32 [2048, 8], P('ep'), may hold values from 0.05 to 0.5
- expert_ids: int32 [2048, 8], P('ep'), may hold values from 0 to 15, all different within a row; in each aligned block of 128 rows (0 to 127, 128 to 255, ...) at most 72 rows name the same one
- gate_proj: bfloat16 [16, 4096, 1536], P('ep', None, 'etp'), may hold values from -0.09375 to 0.09375
- up_proj: bfloat16 [16, 4096, 1536], P('ep', None, 'etp'), may hold values from -0.09375 to 0.09375
- down_proj: bfloat16 [16, 1536, 4096], P('ep', 'etp'), may hold values from -0.15625 to 0.15625
Outputs:
- layer_out: bfloat16 [2048, 4096], P('ep', 'etp')
- token_grad: bfloat16 [2048, 4096], P('ep', 'etp')
- slot_gate_grad: float32 [2048, 8], P('ep')
The draws below stay inside these ranges and needn't reach their ends.
Inputs may be any that keep to these rules, and one draw needn't show every extreme that they name: `expert_ids`: each row names 8 different experts. Within the rows of one index of ep (aligned blocks of 128 rows) no expert is named by more than 72 rows, and in every draw some expert is named by exactly 72 rows of some block.
All inputs are finite; a program needn't handle non-finite values.
Results may differ from the reference program's by a relative error of at most 0.015.
Values may be sent and summed in bfloat16 or wider, within the bound.
A program may use at most 128 MiB of HBM per device.

```python
import math
import jax
import jax.numpy as jnp
import numpy as np
from jax import lax

D = 4096
HID = 1536
TOP = 8
TOK_DEV = 128
TOKENS = 2048
EXPERTS = 16
HQ = 768
CAP = 72
N_EP = 16
N_ETP = 2


def level_of(own_key, extent, shards, least, top_value):
    def one(dim, blocks):
        steps = jax.random.uniform(jax.random.fold_in(jax.random.fold_in(own_key, 6), dim), (blocks,), jnp.float32, least / len(shards), top_value / len(shards))
        return jnp.repeat(jnp.exp(steps), extent[dim] // blocks).reshape((-1,) + (1,) * (len(extent) - dim - 1))

    gain = one(*shards[0])
    for cut in shards[1:]:
        gain = gain * one(*cut)
    return gain


def deal_out(key, own, number, rows, count, top, bound, slope):
    sequence = jax.random.permutation(key, count)
    crowded, usual = shares(count, rows * top, bound, slope, True), shares(count, rows * top, bound, slope, False)
    places = jnp.arange(count)

    def named(tallies, rotation):
        used = int((tallies > 0).sum())
        fixed = max(1, used // 4)
        shifted = fixed + (places - fixed + rotation * (used - fixed)) % max(1, count - fixed)
        return jnp.zeros((count,), jnp.int32).at[sequence[jnp.where(places < fixed, places, shifted)]].set(jnp.asarray(tallies, jnp.int32))

    tallies = jnp.where(number % 4 == 0, named(crowded, number // 4), named(usual, number - number // 4 - 1))
    mixed = jax.random.permutation(jax.random.fold_in(own, 3), count)
    source_of, receiver = mixed[0:count // 2 * 2:2], mixed[1:count // 2 * 2:2]
    margin = jnp.minimum(tallies[source_of] - 1, bound - tallies[receiver]) // 2
    margin = jnp.where((source_of == sequence[0]) | (receiver == sequence[0]) | (tallies[receiver] == 0), 0, jnp.maximum(margin, 0))
    shifted = jax.random.randint(jax.random.fold_in(own, 4), (count // 2,), 0, 1 << 20) % (margin + 1)
    tallies = tallies.at[source_of].add(-shifted).at[receiver].add(shifted)
    items = jnp.searchsorted(jnp.cumsum(tallies), jnp.arange(rows * top), side="right").astype(jnp.int32)
    grid = items.reshape(top, rows).T
    grid = grid[jax.random.permutation(jax.random.fold_in(own, 1), rows)]
    rotation = jax.random.randint(jax.random.fold_in(own, 2), (rows, 1), 0, top)
    return jnp.take_along_axis(grid, (jnp.arange(top)[None, :] + rotation) % top, axis=1)


def shares(amount, total, reach, lean, full):
    portions = [(1 << 20) // math.isqrt(standing ** lean) + 1 for standing in range(1, amount + 1)]
    largest = reach if full else min(reach, max(-(-total // amount), total * portions[0] // sum(portions)))
    least = 1 if total - largest >= amount - 1 else 0
    holding, surplus = [largest] + [least] * (amount - 1), total - largest - least * (amount - 1)
    while surplus > 0:
        movable = [i for i in range(1, amount) if holding[i] < largest] or [i for i in range(1, amount) if holding[i] < reach]
        pool, left = sum([portions[i] for i in movable]), surplus
        for i in movable:
            addition = min(reach - holding[i], max(1, left * portions[i] // pool), surplus)
            holding[i] = holding[i] + addition
            surplus = surplus - addition
    return np.array(holding)


def normal_values(key, shape, width, limit, cuts=(), held_as=jnp.bfloat16):
    values = jax.random.normal(key, shape, jnp.float32) * width
    if len(cuts) > 0:
        values = level_of(key, shape, cuts, -0.22, 0.18) * values
    return jnp.clip(values, min=-limit, max=limit).astype(held_as)


def setup_inputs(seed: int = 0) -> dict:
    seeds = jax.random.split(jax.random.key(seed), 8)
    tokens = normal_values(seeds[0], (TOKENS, D), 1.0, 6.0, ((0, 16), (1, 2)))
    grad_out = normal_values(seeds[1], (TOKENS, D), 0.25, 1.5, ((0, 16), (1, 2)))
    gates = jnp.clip(jnp.exp(math.log(0.5) - 2.3025851 * jax.random.uniform(seeds[2], (TOKENS, TOP), jnp.float32) ** level_of(seeds[2], (TOKENS, TOP), ((0, 16),), -0.2, 0.2)), 0.05, 0.5)
    expert_ids_keys = jax.random.split(jax.random.fold_in(seeds[3], 1), TOKENS // TOK_DEV)
    expert_ids_turns = jax.random.permutation(jax.random.fold_in(seeds[3], 3), TOKENS // TOK_DEV)
    expert_ids = jax.vmap(lambda own, number: deal_out(jax.random.fold_in(seeds[3], 2), own, number, TOK_DEV, EXPERTS, TOP, CAP, 1))(expert_ids_keys, expert_ids_turns).reshape((TOKENS, TOP))
    gate_proj = normal_values(seeds[4], (EXPERTS, D, HID), D ** -0.5, 0.09375, ((0, 16), (2, 2)))
    up_proj = normal_values(seeds[5], (EXPERTS, D, HID), D ** -0.5, 0.09375, ((0, 16), (2, 2)))
    down_proj = normal_values(seeds[6], (EXPERTS, HID, D), HID ** -0.5, 0.15625, ((0, 16), (1, 2)))
    return dict(tokens=tokens, grad_out=grad_out, gates=gates, expert_ids=expert_ids, gate_proj=gate_proj, up_proj=up_proj, down_proj=down_proj)


def reference(tokens, grad_out, gates, expert_ids, gate_proj, up_proj, down_proj):
    rows_total = TOKENS * TOP
    slots_all = N_EP * CAP
    flat_ids = expert_ids.reshape(N_EP, TOK_DEV * TOP)
    onehot = (flat_ids[:, :, None] == jnp.arange(EXPERTS, dtype=jnp.int32)[None, None, :]).astype(jnp.int32)
    before = jnp.cumsum(onehot, axis=1) - onehot
    slot_pos = jnp.sum(before * onehot, axis=2)
    source = jnp.arange(N_EP, dtype=jnp.int32)[:, None]
    target = (flat_ids * slots_all + source * CAP + slot_pos).reshape(rows_total).astype(jnp.int32)
    row_table = jnp.full((EXPERTS * slots_all,), rows_total, jnp.int32)
    row_table = row_table.at[target].set(jnp.arange(rows_total, dtype=jnp.int32)).reshape(EXPERTS, slots_all)
    gate_flat = gates.reshape(rows_total)

    def one_expert(expert):
        copy_idx = row_table[expert]
        is_live = copy_idx < rows_total
        safe_idx = jnp.minimum(copy_idx, rows_total - 1)
        token_idx = safe_idx // TOP
        token_rows = jnp.where(is_live[:, None], tokens[token_idx], jnp.zeros((), tokens.dtype))
        gate_rows = jnp.where(is_live, gate_flat[safe_idx], jnp.zeros((), jnp.float32))
        signal = (gate_rows[:, None] * grad_out[token_idx].astype(jnp.float32)).astype(jnp.bfloat16)
        gate_mat = gate_proj[expert]
        up_mat = up_proj[expert]
        down_mat = down_proj[expert]
        gate_pre = jnp.dot(token_rows, gate_mat, preferred_element_type=jnp.float32)
        up_pre = jnp.dot(token_rows, up_mat, preferred_element_type=jnp.float32)
        sigmoid_gate = jax.nn.sigmoid(gate_pre)
        hidden = (gate_pre * sigmoid_gate * up_pre).astype(jnp.bfloat16)
        grouped = hidden.astype(jnp.float32).reshape(slots_all, N_ETP, HQ)
        down_grouped = down_mat.astype(jnp.float32).reshape(N_ETP, HQ, D)
        part_out = jnp.einsum("rgh,ghd->rgd", grouped, down_grouped).astype(jnp.bfloat16)
        part_out = lax.optimization_barrier(part_out)
        copy_out = jnp.sum(part_out.astype(jnp.float32), axis=1).astype(jnp.bfloat16)
        hidden_grad = jnp.dot(signal, down_mat.T, preferred_element_type=jnp.float32)
        gate_grad = (hidden_grad * up_pre * sigmoid_gate * (1.0 + gate_pre * (1.0 - sigmoid_gate))).astype(jnp.bfloat16)
        up_grad = (hidden_grad * gate_pre * sigmoid_gate).astype(jnp.bfloat16)
        gate_groups = gate_grad.astype(jnp.float32).reshape(slots_all, N_ETP, HQ)
        up_groups = up_grad.astype(jnp.float32).reshape(slots_all, N_ETP, HQ)
        gate_cols = gate_mat.astype(jnp.float32).reshape(D, N_ETP, HQ)
        up_cols = up_mat.astype(jnp.float32).reshape(D, N_ETP, HQ)
        part_in = jnp.einsum("rgh,dgh->rgd", gate_groups, gate_cols) + jnp.einsum("rgh,dgh->rgd", up_groups, up_cols)
        part_in = lax.optimization_barrier(part_in.astype(jnp.bfloat16))
        copy_in = jnp.sum(part_in.astype(jnp.float32), axis=1).astype(jnp.bfloat16)
        return copy_out, copy_in

    out_all, in_all = lax.map(one_expert, jnp.arange(EXPERTS, dtype=jnp.int32))
    out_flat = out_all.reshape(EXPERTS * slots_all, D)
    in_flat = in_all.reshape(EXPERTS * slots_all, D)
    target_tok = target.reshape(TOKENS, TOP)
    mixed = jnp.zeros((TOKENS, D), jnp.float32)
    input_grad = jnp.zeros((TOKENS, D), jnp.float32)
    grad_wide = grad_out.astype(jnp.float32)
    scores = []
    for slot_num in range(TOP):
        copy_out = out_flat[target_tok[:, slot_num]].astype(jnp.float32)
        mixed = mixed + gates[:, slot_num:slot_num + 1] * copy_out
        input_grad = input_grad + in_flat[target_tok[:, slot_num]].astype(jnp.float32)
        scores.append(jnp.sum(grad_wide * copy_out, axis=1))
    return mixed.astype(jnp.bfloat16), input_grad.astype(jnp.bfloat16), jnp.stack(scores, axis=1)
```

```python
import functools
import math

import jax
import jax.numpy as jnp
import numpy as np
from jax import lax
from jax.experimental import pallas as pl
from jax.experimental.pallas import tpu as pltpu
from jax.sharding import PartitionSpec as P

BF = jnp.bfloat16
F32 = jnp.float32
MESH = pl.DeviceIdType.MESH


class Place:
    def __init__(self, ring, groups):
        self.ring, self.groups = ring, groups
        self.depth = math.gcd(ring, 4)
        self.cols = ring // self.depth
        me = lax.axis_index("ep")
        self.g = lax.axis_index("etp")
        self.core = lax.rem(me, 2)
        chip = me // 2
        x, z = lax.rem(chip, self.cols), chip // self.cols
        self.p = x * self.depth + z + lax.rem(x, 2) * (self.depth - 1 - 2 * z)

    def at(self, offset):
        return lax.rem(self.p + offset + self.ring, self.ring)

    def chip(self, offset):
        pos = self.at(offset)
        x, t = pos // self.depth, lax.rem(pos, self.depth)
        z = t + lax.rem(x, 2) * (self.depth - 1 - 2 * t)
        return ((z * self.cols + x) * 2 + self.core, self.g)

    def sibling(self):
        return (lax.axis_index("ep") + 1 - 2 * self.core, self.g)

    def group(self, j):
        return lax.rem(self.g + j, self.groups)

    def partner(self, j):
        return (lax.axis_index("ep"), self.group(j))

    def greet(self, with_sibling):
        barrier = pltpu.get_barrier_semaphore()
        others = [self.chip(1), self.chip(-1)] + [self.partner(j) for j in range(1, self.groups)]
        if with_sibling:
            others.append(self.sibling())
        for other in others:
            pl.semaphore_signal(barrier, inc=1, device_id=other, device_id_type=MESH)
        pl.semaphore_wait(barrier, len(others))


def remote(src, dst, send, recv, where):
    return pltpu.make_async_remote_copy(
        src_ref=src, dst_ref=dst, send_sem=send, recv_sem=recv, device_id=where, device_id_type=MESH
    )


def gather_kernel(
    ring, groups, tok_ref, grad_ref, tok, tok_sib, grad, grad_sib, local_sem, first, rings, fans, late
):
    at = Place(ring, groups)
    at.greet(True)
    g = at.g
    sib = at.sibling()
    own_tok = pltpu.make_async_copy(tok_ref, tok.at[g, at.p], local_sem.at[0])
    own_grad = pltpu.make_async_copy(grad_ref, grad.at[g, at.p], local_sem.at[1])
    own_tok.start()
    own_grad.start()
    heads = []
    for j in range(1, groups):
        head = remote(
            grad_ref, grad.at[g, at.p], first.at[0, j - 1], first.at[1, j - 1], at.partner(j)
        )
        head.start()
        heads.append(head)
    own_tok.wait()

    def back(d, s):
        return at.at(-s if d == 0 else s)

    fan_y, fan_s, fan_t = {}, {}, {}

    def fan_tok(s):
        for d in range(2):
            b = back(d, s)
            fan_y[s, d] = []
            for j in range(1, groups):
                c = remote(
                    tok.at[g, b, d],
                    tok.at[g, b, d],
                    fans.at[0, j, d, s],
                    fans.at[1, j, d, s],
                    at.partner(j),
                )
                c.start()
                fan_y[s, d].append(c)

    def fan_grad(s):
        for d in range(2):
            b = back(d, s)
            c = remote(
                grad.at[:, b, d], grad_sib.at[:, b, d], fans.at[0, 0, d, s], fans.at[1, 0, d, s], sib
            )
            c.start()
            fan_s[s, d] = c

    def fan_late(s):
        for d in range(2):
            b = back(d, s)
            for c in fan_y[s, d]:
                c.wait_recv()
            c = remote(tok.at[:, b, d], tok_sib.at[:, b, d], late.at[0, d, s], late.at[1, d, s], sib)
            c.start()
            fan_t[s, d] = c

    hops = {}

    def hop(kind, d, s):
        b = back(d, s - 1)
        block = tok.at[g, b, d] if kind == 0 else grad.at[:, b, d]
        if s > 1:
            hops[kind, d, s - 1].wait_recv()
        if s < ring:
            c = remote(
                block,
                block,
                rings.at[0, kind, d, s - 1],
                rings.at[1, kind, d, s - 1],
                at.chip(1 if d == 0 else -1),
            )
            c.start()
            hops[kind, d, s] = c

    for s in range(1, ring + 1):
        hop(0, 0, s)
        hop(0, 1, s)
        if s == 1:
            own_grad.wait()
            for head in heads:
                head.wait_recv()
        if s < ring:
            fan_tok(s - 1)
        hop(1, 0, s)
        hop(1, 1, s)
        if s < ring:
            fan_grad(s - 1)
        if s >= 2:
            fan_late(s - 2)
    fan_tok(ring - 1)
    fan_grad(ring - 1)
    fan_late(ring - 1)
    for c in list(fan_s.values()) + list(fan_t.values()):
        c.wait()
    for group in fan_y.values():
        for c in group:
            c.wait_send()
    for c in list(hops.values()) + heads:
        c.wait_send()


def gather(tokens, grad_out, ring, groups):
    rows, width = tokens.shape
    half = rows // 2
    full = jax.ShapeDtypeStruct((groups, ring, 2, half, width), BF)
    dma = pltpu.SemaphoreType.DMA
    hbm = pl.BlockSpec(memory_space=pltpu.HBM)
    return pl.pallas_call(
        functools.partial(gather_kernel, ring, groups),
        out_shape=(full,) * 4,
        in_specs=[hbm, hbm],
        out_specs=(hbm,) * 4,
        scratch_shapes=[
            dma((2,)),
            dma((2, groups - 1)),
            dma((2, 2, 2, ring - 1)),
            dma((2, groups, 2, ring)),
            dma((2, 2, ring)),
        ],
        compiler_params=pltpu.CompilerParams(collective_id=0, has_side_effects=True),
    )(tokens.reshape(2, half, width), grad_out.reshape(2, half, width))


def scatter_kernel(
    ring, groups, s_out, s_in, res_out, res_in, v_out, v_in, r_out, r_in, y_in, y_out, loads, rings, ys, tail
):
    at = Place(ring, groups)
    g = at.g
    half = v_in.shape[2]

    def dest(d, s):
        return at.at(-s if d == 0 else s)

    load_out, load_in, swap = {}, {}, {}
    for s in range(1, ring + 1):
        for d in range(2):
            b = dest(d, s)
            load_out[s, d] = pltpu.make_async_copy(
                s_out.at[:, b, d], v_out.at[:, b, d], loads.at[0, d, s - 1]
            )
            load_in[s, d] = pltpu.make_async_copy(s_in.at[g, b, d], v_in.at[b, d], loads.at[1, d, s - 1])
            load_out[s, d].start()
            load_in[s, d].start()
    at.greet(False)
    for s in range(1, ring + 1):
        for d in range(2):
            b = dest(d, s)
            swap[s, d] = []
            for j in range(1, groups):
                c = remote(
                    s_in.at[at.group(j), b, d],
                    y_in.at[j - 1, b, d],
                    ys.at[0, j - 1, d, s - 1],
                    ys.at[1, j - 1, d, s - 1],
                    at.partner(j),
                )
                c.start()
                swap[s, d].append(c)

    def total(target, others):
        @pl.loop(0, half // 16)
        def _(i):
            rows = pl.ds(pl.multiple_of(i * 16, 16), 16)
            acc = target[rows, :].astype(F32)
            for other in others:
                acc = acc + other[rows, :].astype(F32)
            target[rows, :] = acc.astype(BF)

    hop_out, hop_in = {}, {}
    for s in range(1, ring + 1):
        for d in range(2):
            b = dest(d, s)
            load_out[s, d].wait()
            if s > 1:
                hop_out[s - 1, d].wait_recv()
                for q in range(groups):
                    total(v_out.at[q, b, d], [r_out.at[d, s - 2, q]])
            if s < ring:
                c = remote(
                    v_out.at[:, b, d],
                    r_out.at[d, s - 1],
                    rings.at[0, 0, d, s - 1],
                    rings.at[1, 0, d, s - 1],
                    at.chip(1 if d == 0 else -1),
                )
                c.start()
                hop_out[s, d] = c
        if s == ring:
            ends = []
            for d in range(2):
                for j in range(1, groups):
                    c = remote(
                        v_out.at[at.group(j), at.p, d],
                        y_out.at[j - 1, d],
                        tail.at[0, j - 1, d],
                        tail.at[1, j - 1, d],
                        at.partner(j),
                    )
                    c.start()
                    ends.append(c)
        for d in range(2):
            b = dest(d, s)
            load_in[s, d].wait()
            others = []
            for c in swap[s, d]:
                c.wait_recv()
            others = [y_in.at[j - 1, b, d] for j in range(1, groups)]
            if s > 1:
                hop_in[s - 1, d].wait_recv()
                others.append(r_in.at[d, s - 2])
            total(v_in.at[b, d], others)
            if s < ring:
                c = remote(
                    v_in.at[b, d],
                    r_in.at[d, s - 1],
                    rings.at[0, 1, d, s - 1],
                    rings.at[1, 1, d, s - 1],
                    at.chip(1 if d == 0 else -1),
                )
                c.start()
                hop_in[s, d] = c
    for d in range(2):
        res_in[d] = v_in[at.p, d]
    for c in ends:
        c.wait_recv()
    for d in range(2):
        total(v_out.at[g, at.p, d], [y_out.at[j - 1, d] for j in range(1, groups)])
        res_out[d] = v_out[g, at.p, d]
    for c in list(hop_out.values()) + list(hop_in.values()) + ends:
        c.wait_send()
    for group in swap.values():
        for c in group:
            c.wait_send()


def scatter(s_out, s_in):
    groups, ring, _, half, width = s_out.shape
    res = jax.ShapeDtypeStruct((2, half, width), BF)
    dma = pltpu.SemaphoreType.DMA
    hbm = pl.BlockSpec(memory_space=pltpu.HBM)
    vmem = pl.BlockSpec(memory_space=pltpu.VMEM)
    out, inn = pl.pallas_call(
        functools.partial(scatter_kernel, ring, groups),
        out_shape=(res, res),
        in_specs=[hbm, hbm],
        out_specs=(vmem, vmem),
        scratch_shapes=[
            pltpu.VMEM((groups, ring, 2, half, width), BF),
            pltpu.VMEM((ring, 2, half, width), BF),
            pltpu.VMEM((2, ring - 1, groups, half, width), BF),
            pltpu.VMEM((2, ring - 1, half, width), BF),
            pltpu.VMEM((groups - 1, ring, 2, half, width), BF),
            pltpu.VMEM((groups - 1, 2, half, width), BF),
            dma((2, 2, ring)),
            dma((2, 2, 2, ring - 1)),
            dma((2, groups - 1, 2, ring)),
            dma((2, groups - 1, 2)),
        ],
        compiler_params=pltpu.CompilerParams(
            collective_id=1, has_side_effects=True, vmem_limit_bytes=60 << 20
        ),
    )(s_out, s_in)
    return out.reshape(2 * half, width), inn.reshape(2 * half, width)


def dot(a, b):
    return lax.dot_general(a, b, (((1,), (0,)), ((), ())), preferred_element_type=F32)


def dot_t(a, b):
    return lax.dot_general(a, b, (((1,), (1,)), ((), ())), preferred_element_type=F32)


def expert_kernel(groups, adding, gate_ref, tok, grad, gate_w, up_w, down_w, *rest):
    if adding:
        add_out, add_in, out, inn, score = rest
    else:
        out, inn, score = rest
    width = tok.shape[2]
    cuts = [slice(g * width, (g + 1) * width) for g in range(groups)]
    gate_pre = sum(dot(tok[g], gate_w[cuts[g], :]) for g in range(groups))
    up_pre = sum(dot(tok[g], up_w[cuts[g], :]) for g in range(groups))
    raw = sum(dot_t(grad[g], down_w[:, cuts[g]]) for g in range(groups))
    gate = gate_ref[...]
    sig = jax.nn.sigmoid(gate_pre)
    act = gate_pre * sig
    hidden = act * up_pre
    score[...] = jnp.sum(hidden * raw, axis=1, keepdims=True)
    hidden = (hidden * gate).astype(BF)
    back = raw * gate
    gate_grad = (back * up_pre * sig * (1.0 + gate_pre * (1.0 - sig))).astype(BF)
    up_grad = (back * act).astype(BF)
    for g in range(groups):
        res = dot(hidden, down_w[:, cuts[g]])
        if adding:
            res = res + add_out[g].astype(F32)
        out[g] = res.astype(BF)
        res = dot_t(gate_grad, gate_w[cuts[g], :]) + dot_t(up_grad, up_w[cuts[g], :])
        if adding:
            res = res + add_in[g].astype(F32)
        inn[g] = res.astype(BF)


def expert(gate, tok, grad, gate_proj, up_proj, down_proj, added=()):
    groups, count, width = tok.shape
    tile = 256
    slab = pl.BlockSpec((groups, tile, width), lambda i: (0, i, 0))
    column = pl.BlockSpec((tile, 1), lambda i: (i, 0))

    def fixed(w):
        return pl.BlockSpec((None,) + w.shape[1:], lambda i: (0, 0, 0), pipeline_mode=pl.Buffered(1))

    full = jax.ShapeDtypeStruct(tok.shape, BF)
    hid = gate_proj.shape[2]
    return pl.pallas_call(
        functools.partial(expert_kernel, groups, bool(added)),
        grid=(count // tile,),
        out_shape=(full, full, jax.ShapeDtypeStruct((count, 1), F32)),
        in_specs=[column, slab, slab, fixed(gate_proj), fixed(up_proj), fixed(down_proj)]
        + [slab] * len(added),
        out_specs=(slab, slab, column),
        input_output_aliases={6: 0, 7: 1} if added else {},
        cost_estimate=pl.CostEstimate(
            flops=12 * count * groups * width * hid, bytes_accessed=8 * count * groups * width, transcendentals=count * hid
        ),
        compiler_params=pltpu.CompilerParams(vmem_limit_bytes=60 << 20),
    )(gate, tok, grad, gate_proj, up_proj, down_proj, *added)


def local(tokens, grad_out, gates, expert_ids, gate_proj, up_proj, down_proj):
    rows, width = tokens.shape
    groups = lax.axis_size("etp")
    experts = lax.axis_size("ep")
    ring = experts // 2
    core = lax.rem(lax.axis_index("ep"), 2)
    depth = math.gcd(ring, 4)
    cols = ring // depth
    order = np.zeros(ring, np.int32)
    for pos in range(ring):
        x, t = pos // depth, pos % depth
        order[pos] = (t if x % 2 == 0 else depth - 1 - t) * cols + x
    inverse = np.argsort(order)
    count = ring * rows

    onehot = expert_ids[:, :, None] == jnp.arange(experts, dtype=jnp.int32)[None, None, :]
    table = jnp.sum(jnp.where(onehot, gates[:, :, None], 0.0), axis=1)
    mine = lax.all_to_all(table.T, "ep", split_axis=0, concat_axis=0, tiled=True)
    mine = mine.reshape(ring, 2, rows)
    mine = jnp.stack([mine[int(c)] for c in order]).transpose(1, 0, 2)
    mine = jnp.where(core == 0, mine, mine[::-1])

    tok_own, tok_sib, grad_own, grad_sib = gather(tokens, grad_out, ring, groups)
    flat = (groups, count, width)
    swap = [(i, i ^ 1) for i in range(experts)]
    weights = (gate_proj, up_proj, down_proj)
    out, inn, score_sib = expert(
        mine[1].reshape(count, 1), tok_sib.reshape(flat), grad_sib.reshape(flat), *weights
    )
    got = (lax.ppermute(out, "ep", swap), lax.ppermute(inn, "ep", swap))
    out, inn, score_own = expert(
        mine[0].reshape(count, 1), tok_own.reshape(flat), grad_own.reshape(flat), *weights, added=got
    )
    scores = [score_own.reshape(ring, rows), score_sib.reshape(ring, rows)]
    shape = (groups, ring, 2, rows // 2, width)
    layer_out, token_grad = scatter(out.reshape(shape), inn.reshape(shape))

    score = jnp.stack(scores)
    score = jnp.where(core == 0, score, score[::-1]).transpose(1, 0, 2)
    score = jnp.stack([score[int(c)] for c in inverse]).reshape(experts, rows)
    score = lax.all_to_all(score, "ep", split_axis=0, concat_axis=0, tiled=True)
    score = lax.psum(score, "etp")
    picked = jnp.sum(jnp.where(onehot, score.T[:, None, :], 0.0), axis=2)
    return layer_out, token_grad, picked


def solution(mesh):
    in_specs = (
        P("ep", "etp"),
        P("ep", "etp"),
        P("ep", None),
        P("ep", None),
        P("ep", None, "etp"),
        P("ep", None, "etp"),
        P("ep", "etp", None),
    )
    out_specs = (P("ep", "etp"), P("ep", "etp"), P("ep", None))
    return jax.shard_map(local, mesh=mesh, in_specs=in_specs, out_specs=out_specs, check_vma=False)
```
